32 devices in a mesh: prow: 4 (over z), pcol: 8 (over y, x, core).
Axes of the slice: x: 2, y: 2, z: 4, core: 2. Of those that a mesh axis runs over, the one named last changes fastest.
Arguments:
- matrix: float32 [2, 4, 256, 8, 256], P(None, 'prow', None, 'pcol'), may hold values from -6 to 6, as said below
Outputs:
- factored: float32 [2, 4, 256, 8, 256], P(None, 'prow', None, 'pcol')
The draws below stay inside these ranges and needn't reach their ends.
Inputs may be any that keep to these rules, and one draw needn't show every extreme that they name: `matrix`: in the first 3 diagonal blocks every diagonal entry lies between 1.3 and 3.2, and diag(1/d) times the off-diagonal part of each such block has spectral norm below about 0.7.
All inputs are finite; a program needn't handle non-finite values.
Results may differ from the reference program's by a relative error of at most 0.0001.
Values sent between devices are 32-bit elements; how exact they have to be, the bound alone decides.
No kernel may reach another device: no remote copies, remote signals or barrier semaphores. Data moves between devices by JAX's collectives and lax.ppermute only.
A program may use at most 64 MiB of HBM per device.

```python
import math
import jax
import jax.numpy as jnp
from jax import lax

B = 256
RB_DEV = 2
PANELS = 3
PROWS = 4
PCOLS = 8


def draw_matrix(key, part):
    first_key, second_key = jax.random.split(key)
    shape = (RB_DEV, PROWS, B, PCOLS, B)
    base = jnp.clip(jax.random.normal(first_key, shape, jnp.float32), -6.0, 6.0)
    block_row = (jnp.arange(RB_DEV)[:, None] * PROWS + jnp.arange(PROWS)[None, :]).reshape(RB_DEV, PROWS, 1, 1, 1)
    block_col = jnp.arange(PCOLS).reshape(1, 1, 1, PCOLS, 1)
    head = (block_row < PANELS) & (block_col < PANELS)
    upper = (block_row < PANELS) & (block_col >= PANELS)
    scale = jnp.where(head, 0.5 / math.sqrt(B), jnp.where(upper, 0.1, 1.0))
    inner_row = jnp.arange(B).reshape(1, 1, B, 1, 1)
    inner_col = jnp.arange(B).reshape(1, 1, 1, 1, B)
    on_diag = head & (block_row == block_col) & (inner_row == inner_col)
    lift = jax.random.uniform(second_key, shape, jnp.float32, 1.5, 3.0)
    return base * scale + jnp.where(on_diag, lift, 0.0)


def setup_inputs(seed: int = 0) -> dict:
    keys = jax.random.split(jax.random.key(seed), 2)
    matrix = draw_matrix(jax.random.fold_in(keys[1], 71), 0)
    return {"matrix": matrix}


def invert(block):
    scales = 1.0 / jnp.diagonal(block)
    first = 2.0 * jnp.diag(scales) - scales[:, None] * block * scales[None, :]
    inner = jnp.dot(block, first, precision=lax.Precision.HIGHEST)
    return 2.0 * first - jnp.dot(first, inner, precision=lax.Precision.HIGHEST)


def reference(matrix):
    shape = matrix.shape
    full = matrix.reshape(shape[0] * shape[1] * shape[2], shape[3] * shape[4])
    for panel in range(PANELS):
        lower = panel * B
        upper = lower + B
        inverse = invert(full[lower:upper, lower:upper])
        factors = jnp.dot(full[upper:, lower:upper], inverse, precision=lax.Precision.HIGHEST)
        update = jnp.dot(factors, full[lower:upper, upper:], precision=lax.Precision.HIGHEST)
        full = full.at[upper:, upper:].set(full[upper:, upper:] - update)
        full = full.at[upper:, lower:upper].set(factors)
        full = full.at[lower:upper, lower:upper].set(inverse)
    return full.reshape(shape)
```

```python
import functools

import jax
import jax.numpy as jnp
from jax import lax
from jax.experimental import pallas as pl
from jax.experimental.pallas import tpu as pltpu
from jax.sharding import PartitionSpec as P

PANELS = 3


def split(value):
    high = value.astype(jnp.bfloat16)
    low = (value - high.astype(jnp.float32)).astype(jnp.bfloat16)
    return high, low


def product(left, right):
    dot = functools.partial(jnp.dot, preferred_element_type=jnp.float32)
    return dot(left[0], right[0]) + (dot(left[0], right[1]) + dot(left[1], right[0]))


def invert(block):
    size = block.shape[0]
    eye = lax.broadcasted_iota(jnp.int32, (size, size), 0) == lax.broadcasted_iota(jnp.int32, (size, size), 1)
    diagonal = jnp.where(eye, block, 0.0)
    down = 1.0 / jnp.sum(diagonal, axis=1, keepdims=True)
    along = 1.0 / jnp.sum(diagonal, axis=0, keepdims=True)
    first = jnp.where(eye, 2.0 * down, 0.0) - down * block * along
    parts = split(first)
    inner = product(split(block), parts)
    return 2.0 * first - product(parts, split(inner))


def distance_groups(row_count):
    groups = []
    for distance in range(1, row_count):
        targets = {(k + distance) % row_count for k in range(PANELS)}
        for group in groups:
            if not targets & group[1]:
                group[0].append(distance)
                group[1].update(targets)
                break
        else:
            groups.append(([distance], targets))
    return [group[0] for group in groups]


def factor_kernel(tile, near, far, own_mine, own_other, far_mine, far_other, near_mine, near_other, out, work):
    count, size = tile.shape[0], tile.shape[2]
    row_count = lax.axis_size("prow")
    my_row = lax.axis_index("prow")
    my_col = lax.axis_index("pcol")
    even = lax.rem(my_col, 2) == 0

    def column(index):
        return slice(index * size, (index + 1) * size)

    def place(target, mine, other, piece, own):
        work[target, :, column(PANELS)] = own

        @pl.when(even)
        def _():
            work[target, :, column(0)] = mine[0, piece]
            work[target, :, column(1)] = other[0, piece]
            work[target, :, column(2)] = mine[1, piece]

        @pl.when(jnp.logical_not(even))
        def _():
            work[target, :, column(0)] = other[0, piece]
            work[target, :, column(1)] = mine[0, piece]
            work[target, :, column(2)] = other[1, piece]

    for index in range(count):
        place(PANELS + index, own_mine, own_other, index, tile[index])

    @pl.when(my_row < PANELS)
    def _():
        place(my_row, own_mine, own_other, 0, tile[0])

    for number, group in enumerate(distance_groups(row_count)):
        for distance in group:
            source = lax.rem(my_row + row_count - distance, row_count)

            @pl.when(source < PANELS)
            def _():
                if number == 0:
                    place(source, near_mine, near_other, 0, near[0])
                else:
                    place(source, far_mine, far_other, number - 1, far[number - 1])

    for panel in range(PANELS):
        inverse = invert(work[panel, :, column(panel)])
        work[panel, :, column(panel)] = inverse
        inverse = split(inverse)
        rest = slice((panel + 1) * size, (PANELS + 1) * size)
        pivot_row = split(work[panel, :, rest])
        for index in range(panel + 1, PANELS + count):
            factor = product(split(work[index, :, column(panel)]), inverse)
            work[index, :, column(panel)] = factor
            work[index, :, rest] = work[index, :, rest] - product(split(factor), pivot_row)

    at = jnp.where(my_col < PANELS, my_col, PANELS)
    columns = pl.ds(pl.multiple_of(at * size, size), size)
    first = jnp.where(my_row < PANELS, my_row, PANELS)
    out[0] = work[first, :, columns]
    for index in range(1, count):
        out[index] = work[PANELS + index, :, columns]


def factor(operands, count, size):
    return pl.pallas_call(
        factor_kernel,
        out_shape=jax.ShapeDtypeStruct((count, size, size), jnp.float32),
        in_specs=[pl.BlockSpec(memory_space=pltpu.VMEM)] * len(operands),
        out_specs=pl.BlockSpec(memory_space=pltpu.VMEM),
        scratch_shapes=[pltpu.VMEM((PANELS + count, size, (PANELS + 1) * size), jnp.float32)],
        compiler_params=pltpu.CompilerParams(vmem_limit_bytes=56 * 1024 * 1024),
    )(*operands)


def spread(block):
    col_count = lax.axis_size("pcol")
    sources = range(PANELS)
    arrived = {0: block}
    for mask in range(2, col_count, 2):
        top = 1 << (mask.bit_length() - 1)
        before = mask ^ top
        arrived[mask] = lax.ppermute(arrived[before], "pcol", [(c ^ before, c ^ mask) for c in sources])
    chip = lax.axis_index("pcol") // 2
    same = lax.select_n(chip, *[arrived[2 * index] for index in range(col_count // 2)])
    third = lax.select_n(chip ^ 1, *[arrived[2 * index] for index in range(col_count // 2)])
    mine = jnp.stack([same, third])
    other = lax.ppermute(mine, "pcol", [(c, c ^ 1) for c in range(col_count)])
    return mine, other


def body(matrix):
    shape = matrix.shape
    tile = matrix.reshape(shape[0], shape[2], shape[4])
    row_count = lax.axis_size("prow")
    own = spread(tile)
    rows = [
        sum(lax.ppermute(tile[0], "prow", [(k, (k + d) % row_count) for k in range(PANELS)]) for d in group)
        for group in distance_groups(row_count)
    ]
    far = jnp.stack(rows[1:])
    near = rows[0][None]
    operands = (tile, near, far, *own, *spread(far), *spread(near))
    return factor(operands, shape[0], shape[2]).reshape(shape)


def solution(mesh):
    return jax.shard_map(
        body,
        mesh=mesh,
        in_specs=(P(None, "prow", None, "pcol", None),),
        out_specs=P(None, "prow", None, "pcol", None),
        check_vma=False,
    )
```

```python
import functools
import math

import jax
import jax.numpy as jnp
from jax import lax
from jax.experimental import pallas as pl
from jax.experimental.pallas import tpu as pltpu
from jax.sharding import PartitionSpec as P


PANELS = 3


def split(value):
    high = value.astype(jnp.bfloat16)
    low = (value - high.astype(jnp.float32)).astype(jnp.bfloat16)
    return high, low


def product(left, right):
    dot = functools.partial(jnp.dot, preferred_element_type=jnp.float32)
    return dot(left[0], right[0]) + (dot(left[0], right[1]) + dot(left[1], right[0]))


def invert(block):
    size = block.shape[0]
    eye = lax.broadcasted_iota(jnp.int32, (size, size), 0) == lax.broadcasted_iota(jnp.int32, (size, size), 1)
    diagonal = jnp.where(eye, block, 0.0)
    down = 1.0 / jnp.sum(diagonal, axis=1, keepdims=True)
    along = 1.0 / jnp.sum(diagonal, axis=0, keepdims=True)
    first = jnp.where(eye, 2.0 * down, 0.0) - down * block * along
    parts = split(first)
    inner = product(split(block), parts)
    return 2.0 * first - product(parts, split(inner))


def distance_groups(row_count):
    groups = []
    for distance in range(1, row_count):
        targets = {(k + distance) % row_count for k in range(PANELS)}
        for group in groups:
            if not targets & group[1]:
                group[0].append(distance)
                group[1].update(targets)
                break
        else:
            groups.append(([distance], targets))
    groups = [group[0] for group in groups]
    return groups[:1] + groups[2:], groups[1]


LANES = 128


def load(ref, index, size):
    step = size // LANES
    return jnp.concatenate([ref[(*index, pl.ds(part, size, stride=step), slice(None))] for part in range(step)], axis=1)


def store(ref, index, value):
    size = value.shape[0]
    step = size // LANES
    for part in range(step):
        ref[(*index, pl.ds(part, size, stride=step), slice(None))] = value[:, part * LANES : (part + 1) * LANES]


def factor_kernel(size, tile, near, far, own_mine, own_other, far_mine, far_other, near_mine, near_other, out, work):
    count = tile.shape[0]
    row_count = lax.axis_size("prow")
    my_row = lax.axis_index("prow")
    my_col = lax.axis_index("pcol")
    even = lax.rem(my_col, 2) == 0

    def column(index):
        return slice(index * size, (index + 1) * size)

    def place(target, mine, other, piece, own, own_index):
        work[target, :, column(PANELS)] = load(own, (own_index,), size)

        @pl.when(even)
        def _():
            work[target, :, column(0)] = load(mine, (0, piece), size)
            work[target, :, column(1)] = load(other, (0, piece), size)
            work[target, :, column(2)] = load(mine, (1, piece), size)

        @pl.when(jnp.logical_not(even))
        def _():
            work[target, :, column(0)] = load(other, (0, piece), size)
            work[target, :, column(1)] = load(mine, (0, piece), size)
            work[target, :, column(2)] = load(other, (1, piece), size)

    for index in range(count):
        place(PANELS + index, own_mine, own_other, index, tile, index)

    @pl.when(my_row < PANELS)
    def _():
        place(my_row, own_mine, own_other, 0, tile, 0)

    far_groups, near_group = distance_groups(row_count)
    for number, group in enumerate([near_group] + far_groups):
        for distance in group:
            source = lax.rem(my_row + row_count - distance, row_count)

            @pl.when(source < PANELS)
            def _():
                if number == 0:
                    place(source, near_mine, near_other, 0, near, 0)
                else:
                    place(source, far_mine, far_other, number - 1, far, number - 1)

    for panel in range(PANELS):
        inverse = invert(work[panel, :, column(panel)])
        work[panel, :, column(panel)] = inverse
        inverse = split(inverse)
        rest = slice((panel + 1) * size, (PANELS + 1) * size)
        pivot_row = split(work[panel, :, rest])
        for index in range(panel + 1, PANELS + count):
            factor = product(split(work[index, :, column(panel)]), inverse)
            work[index, :, column(panel)] = factor
            work[index, :, rest] = work[index, :, rest] - product(split(factor), pivot_row)

    at = jnp.where(my_col < PANELS, my_col, PANELS)
    columns = pl.ds(pl.multiple_of(at * size, size), size)
    first = jnp.where(my_row < PANELS, my_row, PANELS)
    store(out, (0,), work[first, :, columns])
    for index in range(1, count):
        store(out, (index,), work[PANELS + index, :, columns])


def in_vmem(kernel, out_shape, operands, scratch=(), spare=4):
    words = sum(operand.size for operand in operands) + math.prod(out_shape) + sum(math.prod(s.shape) for s in scratch)
    return pl.pallas_call(
        kernel,
        out_shape=jax.ShapeDtypeStruct(out_shape, jnp.float32),
        in_specs=[pl.BlockSpec(memory_space=pltpu.VMEM)] * len(operands),
        out_specs=pl.BlockSpec(memory_space=pltpu.VMEM),
        scratch_shapes=list(scratch),
        compiler_params=pltpu.CompilerParams(vmem_limit_bytes=4 * words + spare * 1024 * 1024),
    )(*operands)


def factor(operands, size):
    count = operands[0].shape[0]
    work = pltpu.VMEM((PANELS + count, size, (PANELS + 1) * size), jnp.float32)
    return in_vmem(functools.partial(factor_kernel, size), operands[0].shape, operands, [work], 16)


def pick_kernel(*refs):
    sources, mine = refs[:-1], refs[-1]
    chip = lax.axis_index("pcol") // 2
    for index, source in enumerate(sources):
        for slot in range(2):

            @pl.when(chip == (index ^ slot))
            def _():
                mine[slot] = source[...]


def arrivals(block):
    arrived = {0: block}
    for mask in range(2, lax.axis_size("pcol"), 2):
        before = mask & (mask - 1)
        arrived[mask] = lax.ppermute(arrived[before], "pcol", [(c ^ before, c ^ mask) for c in range(PANELS)])
    return [arrived[mask] for mask in sorted(arrived)]


def exchange(arrived):
    mine = in_vmem(pick_kernel, (2, *arrived[0].shape), arrived)
    other = lax.ppermute(mine, "pcol", [(c, c ^ 1) for c in range(lax.axis_size("pcol"))])
    return mine, other


def factored(matrix):
    shape = matrix.shape
    size = shape[4]
    tile = matrix.reshape(shape[0], shape[2] * size // LANES, LANES)
    row_count = lax.axis_size("prow")
    far_groups, near_group = distance_groups(row_count)

    def from_rows(block, group):
        total = None
        for d in group:
            arrived = lax.ppermute(block, "prow", [(k, (k + d) % row_count) for k in range(PANELS)])
            total = arrived if total is None else total + arrived
        return total

    rows = [from_rows(tile[:1], group) for group in far_groups]
    own = arrivals(tile)
    late, first = lax.optimization_barrier((tile[:1], rows[0]))
    near = from_rows(late, near_group)
    far = jnp.concatenate([first] + rows[1:])
    operands = (tile, near, far, *exchange(own), *exchange(arrivals(far)), *exchange(arrivals(near)))
    return factor(operands, size).reshape(shape)


def solution(mesh):
    return jax.shard_map(
        factored,
        mesh=mesh,
        in_specs=(P(None, "prow", None, "pcol", None),),
        out_specs=P(None, "prow", None, "pcol", None),
        check_vma=False,
    )
```

```python
import functools
import math

import jax
import jax.numpy as jnp
from jax import lax
from jax.experimental import pallas as pl
from jax.experimental.pallas import tpu as pltpu
from jax.sharding import PartitionSpec as P


PANELS = 3


def split(value):
    high = value.astype(jnp.bfloat16)
    low = (value - high.astype(jnp.float32)).astype(jnp.bfloat16)
    return high, low


def product(left, right):
    dot = functools.partial(jnp.dot, preferred_element_type=jnp.float32)
    return dot(left[0], right[0]) + (dot(left[0], right[1]) + dot(left[1], right[0]))


def invert(block):
    size = block.shape[0]
    eye = lax.broadcasted_iota(jnp.int32, (size, size), 0) == lax.broadcasted_iota(jnp.int32, (size, size), 1)
    diagonal = jnp.where(eye, block, 0.0)
    down = 1.0 / jnp.sum(diagonal, axis=1, keepdims=True)
    along = 1.0 / jnp.sum(diagonal, axis=0, keepdims=True)
    first = jnp.where(eye, 2.0 * down, 0.0) - down * block * along
    parts = split(first)
    inner = product(split(block), parts)
    return 2.0 * first - product(parts, split(inner))


def distance_groups(row_count):
    groups = []
    for distance in range(1, row_count):
        targets = {(k + distance) % row_count for k in range(PANELS)}
        for group in groups:
            if not targets & group[1]:
                group[0].append(distance)
                group[1].update(targets)
                break
        else:
            groups.append(([distance], targets))
    groups = [group[0] for group in groups]
    return groups[:1] + groups[2:], groups[1]


LANES = 128


def load(ref, index, size):
    step = size // LANES
    return jnp.concatenate([ref[(*index, pl.ds(part, size, stride=step), slice(None))] for part in range(step)], axis=1)


def store(ref, index, value):
    size = value.shape[0]
    step = size // LANES
    for part in range(step):
        ref[(*index, pl.ds(part, size, stride=step), slice(None))] = value[:, part * LANES : (part + 1) * LANES]


def factor_kernel(size, tile, near, far, own_mine, own_other, far_mine, far_other, near_mine, near_other, out, work):
    count = tile.shape[0]
    row_count = lax.axis_size("prow")
    my_row = lax.axis_index("prow")
    my_col = lax.axis_index("pcol")
    even = lax.rem(my_col, 2) == 0

    def column(index):
        return slice(index * size, (index + 1) * size)

    def place(target, mine, other, piece, own, own_index):
        work[target, :, column(PANELS)] = load(own, (own_index,), size)

        @pl.when(even)
        def _():
            work[target, :, column(0)] = load(mine, (0, piece), size)
            work[target, :, column(1)] = load(other, (0, piece), size)
            work[target, :, column(2)] = load(mine, (1, piece), size)

        @pl.when(jnp.logical_not(even))
        def _():
            work[target, :, column(0)] = load(other, (0, piece), size)
            work[target, :, column(1)] = load(mine, (0, piece), size)
            work[target, :, column(2)] = load(other, (1, piece), size)

    for index in range(count):
        place(PANELS + index, own_mine, own_other, index, tile, index)

    @pl.when(my_row < PANELS)
    def _():
        place(my_row, own_mine, own_other, 0, tile, 0)

    far_groups, near_group = distance_groups(row_count)
    for number, group in enumerate([near_group] + far_groups):
        for distance in group:
            source = lax.rem(my_row + row_count - distance, row_count)

            @pl.when(source < PANELS)
            def _():
                if number == 0:
                    place(source, near_mine, near_other, 0, near, 0)
                else:
                    place(source, far_mine, far_other, number - 1, far, number - 1)

    for panel in range(PANELS):
        inverse = invert(work[panel, :, column(panel)])
        work[panel, :, column(panel)] = inverse
        inverse = split(inverse)
        rest = slice((panel + 1) * size, (PANELS + 1) * size)
        pivot_row = split(work[panel, :, rest])
        for index in range(panel + 1, PANELS + count):
            factor = product(split(work[index, :, column(panel)]), inverse)
            work[index, :, column(panel)] = factor
            work[index, :, rest] = work[index, :, rest] - product(split(factor), pivot_row)

    at = jnp.where(my_col < PANELS, my_col, PANELS)
    columns = pl.ds(pl.multiple_of(at * size, size), size)
    first = jnp.where(my_row < PANELS, my_row, PANELS)
    store(out, (0,), work[first, :, columns])
    for index in range(1, count):
        store(out, (index,), work[PANELS + index, :, columns])


def in_vmem(kernel, out_shape, operands, scratch=(), spare=4):
    words = sum(operand.size for operand in operands) + math.prod(out_shape) + sum(math.prod(s.shape) for s in scratch)
    return pl.pallas_call(
        kernel,
        out_shape=jax.ShapeDtypeStruct(out_shape, jnp.float32),
        in_specs=[pl.BlockSpec(memory_space=pltpu.VMEM)] * len(operands),
        out_specs=pl.BlockSpec(memory_space=pltpu.VMEM),
        scratch_shapes=list(scratch),
        compiler_params=pltpu.CompilerParams(vmem_limit_bytes=4 * words + spare * 1024 * 1024),
    )(*operands)


def factor(operands, size):
    count = operands[0].shape[0]
    work = pltpu.VMEM((PANELS + count, size, (PANELS + 1) * size), jnp.float32)
    return in_vmem(functools.partial(factor_kernel, size), operands[0].shape, operands, [work], 16)


def place_on_ring(position):
    return position ^ (position >> 1)


def ring_steps(chips):
    steps = []
    for step in range(chips - 1):
        hops = ((step, step + 1, 0), (-step, -step - 1, 1), (1 - step, -step, 0))
        steps.append(
            [(2 * place_on_ring(a % chips) + core, 2 * place_on_ring(b % chips) + core) for a, b, core in hops]
        )
    return steps


def pick_kernel(*refs):
    sources, mine = refs[:-1], refs[-1]
    chips = len(sources)
    me = lax.axis_index("pcol")
    even = lax.rem(me, 2) == 0
    for position in range(chips):

        @pl.when(me // 2 == place_on_ring(position))
        def _():
            @pl.when(even)
            def _():
                mine[0] = sources[position][...]
                mine[1] = sources[(1 - position) % chips][...]

            @pl.when(jnp.logical_not(even))
            def _():
                mine[0] = sources[-position % chips][...]


def arrivals(block):
    arrived = [block]
    for pairs in ring_steps(lax.axis_size("pcol") // 2):
        arrived.append(lax.ppermute(arrived[-1], "pcol", pairs))
    return arrived


def exchange(arrived):
    mine = in_vmem(pick_kernel, (2, *arrived[0].shape), arrived)
    other = lax.ppermute(mine, "pcol", [(c, c ^ 1) for c in range(lax.axis_size("pcol"))])
    return mine, other


def factored(matrix):
    shape = matrix.shape
    size = shape[4]
    tile = matrix.reshape(shape[0], shape[2] * size // LANES, LANES)
    row_count = lax.axis_size("prow")
    far_groups, near_group = distance_groups(row_count)

    def from_rows(block, group):
        total = None
        for d in group:
            arrived = lax.ppermute(block, "prow", [(k, (k + d) % row_count) for k in range(PANELS)])
            total = arrived if total is None else total + arrived
        return total

    rows = [from_rows(tile[:1], group) for group in far_groups]
    own = arrivals(tile)
    late, first = lax.optimization_barrier((tile[:1], rows[0]))
    near = from_rows(late, near_group)
    far = jnp.concatenate([first] + rows[1:])
    operands = (tile, near, far, *exchange(own), *exchange(arrivals(far)), *exchange(arrivals(near)))
    return factor(operands, size).reshape(shape)


def solution(mesh):
    return jax.shard_map(
        factored,
        mesh=mesh,
        in_specs=(P(None, "prow", None, "pcol", None),),
        out_specs=P(None, "prow", None, "pcol", None),
        check_vma=False,
    )
```

```python
import functools
import math

import jax
import jax.numpy as jnp
from jax import lax
from jax.experimental import pallas as pl
from jax.experimental.pallas import tpu as pltpu
from jax.sharding import PartitionSpec as P


PANELS = 3


def split(value):
    high = value.astype(jnp.bfloat16)
    low = (value - high.astype(jnp.float32)).astype(jnp.bfloat16)
    return high, low


def product(left, right):
    dot = functools.partial(jnp.dot, preferred_element_type=jnp.float32)
    return dot(left[0], right[0]) + (dot(left[0], right[1]) + dot(left[1], right[0]))


def invert(block):
    size = block.shape[0]
    eye = lax.broadcasted_iota(jnp.int32, (size, size), 0) == lax.broadcasted_iota(jnp.int32, (size, size), 1)
    diagonal = jnp.where(eye, block, 0.0)
    down = 1.0 / jnp.sum(diagonal, axis=1, keepdims=True)
    along = 1.0 / jnp.sum(diagonal, axis=0, keepdims=True)
    first = jnp.where(eye, 2.0 * down, 0.0) - down * block * along
    parts = split(first)
    inner = product(split(block), parts)
    return 2.0 * first - product(parts, split(inner))


def distance_groups(row_count):
    groups = []
    for distance in range(1, row_count):
        targets = {(k + distance) % row_count for k in range(PANELS)}
        for group in groups:
            if not targets & group[1]:
                group[0].append(distance)
                group[1].update(targets)
                break
        else:
            groups.append(([distance], targets))
    groups = [group[0] for group in groups]
    return groups[:1] + groups[2:], groups[1]


LANES = 128


def load(ref, index, size):
    step = size // LANES
    return jnp.concatenate([ref[(*index, pl.ds(part, size, stride=step), slice(None))] for part in range(step)], axis=1)


def store(ref, index, value):
    size = value.shape[0]
    step = size // LANES
    for part in range(step):
        ref[(*index, pl.ds(part, size, stride=step), slice(None))] = value[:, part * LANES : (part + 1) * LANES]


def factor_kernel(size, tile, near, far, own_mine, own_other, far_mine, far_other, near_mine, near_other, out, work):
    count = tile.shape[0]
    row_count = lax.axis_size("prow")
    my_row = lax.axis_index("prow")
    my_col = lax.axis_index("pcol")
    even = lax.rem(my_col, 2) == 0

    def column(index):
        return slice(index * size, (index + 1) * size)

    def place(target, mine, other, piece, own, own_index):
        work[target, :, column(PANELS)] = load(own, (own_index,), size)

        @pl.when(even)
        def _():
            work[target, :, column(0)] = load(mine, (0, piece), size)
            work[target, :, column(1)] = load(other, (0, piece), size)
            work[target, :, column(2)] = load(mine, (1, piece), size)

        @pl.when(jnp.logical_not(even))
        def _():
            work[target, :, column(0)] = load(other, (0, piece), size)
            work[target, :, column(1)] = load(mine, (0, piece), size)
            work[target, :, column(2)] = load(other, (1, piece), size)

    for index in range(count):
        place(PANELS + index, own_mine, own_other, index, tile, index)

    @pl.when(my_row < PANELS)
    def _():
        place(my_row, own_mine, own_other, 0, tile, 0)

    far_groups, near_group = distance_groups(row_count)
    for number, group in enumerate([near_group] + far_groups):
        for distance in group:
            source = lax.rem(my_row + row_count - distance, row_count)

            @pl.when(source < PANELS)
            def _():
                if number == 0:
                    place(source, near_mine, near_other, 0, near, 0)
                else:
                    place(source, far_mine, far_other, number - 1, far, number - 1)

    for panel in range(PANELS):
        inverse = invert(work[panel, :, column(panel)])
        work[panel, :, column(panel)] = inverse
        inverse = split(inverse)
        rest = slice((panel + 1) * size, (PANELS + 1) * size)
        pivot_row = split(work[panel, :, rest])
        for index in range(panel + 1, PANELS + count):
            factor = product(split(work[index, :, column(panel)]), inverse)
            work[index, :, column(panel)] = factor
            work[index, :, rest] = work[index, :, rest] - product(split(factor), pivot_row)

    at = jnp.where(my_col < PANELS, my_col, PANELS)
    columns = pl.ds(pl.multiple_of(at * size, size), size)
    first = jnp.where(my_row < PANELS, my_row, PANELS)
    store(out, (0,), work[first, :, columns])
    for index in range(1, count):
        store(out, (index,), work[PANELS + index, :, columns])


def in_vmem(kernel, out_shape, operands, scratch=(), spare=4):
    words = sum(operand.size for operand in operands) + math.prod(out_shape) + sum(math.prod(s.shape) for s in scratch)
    return pl.pallas_call(
        kernel,
        out_shape=jax.ShapeDtypeStruct(out_shape, jnp.float32),
        in_specs=[pl.BlockSpec(memory_space=pltpu.VMEM)] * len(operands),
        out_specs=pl.BlockSpec(memory_space=pltpu.VMEM),
        scratch_shapes=list(scratch),
        compiler_params=pltpu.CompilerParams(vmem_limit_bytes=4 * words + spare * 1024 * 1024),
    )(*operands)


def factor(operands, size):
    count = operands[0].shape[0]
    work = pltpu.VMEM((PANELS + count, size, (PANELS + 1) * size), jnp.float32)
    return in_vmem(functools.partial(factor_kernel, size), operands[0].shape, operands, [work], 16)


def pick_kernel(*refs):
    sources, mine = refs[:-1], refs[-1]
    chip = lax.axis_index("pcol") // 2
    for index, source in enumerate(sources):
        for slot in range(2):

            @pl.when(chip == (index ^ slot))
            def _():
                mine[slot] = source[...]


def relay_kernel(even_ref, odd_ref, out):
    even = lax.rem(lax.axis_index("pcol"), 2) == 0

    @pl.when(even)
    def _():
        out[...] = even_ref[...]

    @pl.when(jnp.logical_not(even))
    def _():
        out[...] = odd_ref[...]


def arrivals(block):
    arrived = {0: block}
    for mask in range(2, lax.axis_size("pcol"), 2):
        before = (mask & (mask - 1), mask ^ (1 << (mask.bit_length() - 1)))
        even, odd = arrived[before[0]], arrived[before[1]]
        payload = even if before[0] == before[1] else in_vmem(relay_kernel, block.shape, [even, odd])
        arrived[mask] = lax.ppermute(payload, "pcol", [(c ^ before[c % 2], c ^ mask) for c in range(PANELS)])
    return [arrived[mask] for mask in sorted(arrived)]


def exchange(arrived):
    mine = in_vmem(pick_kernel, (2, *arrived[0].shape), arrived)
    other = lax.ppermute(mine, "pcol", [(c, c ^ 1) for c in range(lax.axis_size("pcol"))])
    return mine, other


def factored(matrix):
    shape = matrix.shape
    size = shape[4]
    tile = matrix.reshape(shape[0], shape[2] * size // LANES, LANES)
    row_count = lax.axis_size("prow")
    far_groups, near_group = distance_groups(row_count)

    def from_rows(block, group):
        total = None
        for d in group:
            arrived = lax.ppermute(block, "prow", [(k, (k + d) % row_count) for k in range(PANELS)])
            total = arrived if total is None else total + arrived
        return total

    rows = [from_rows(tile[:1], group) for group in far_groups]
    own = arrivals(tile)
    late, first = lax.optimization_barrier((tile[:1], rows[0]))
    near = from_rows(late, near_group)
    far = jnp.concatenate([first] + rows[1:])
    operands = (tile, near, far, *exchange(own), *exchange(arrivals(far)), *exchange(arrivals(near)))
    return factor(operands, size).reshape(shape)


def solution(mesh):
    return jax.shard_map(
        factored,
        mesh=mesh,
        in_specs=(P(None, "prow", None, "pcol", None),),
        out_specs=P(None, "prow", None, "pcol", None),
        check_vma=False,
    )
```

```python
import functools
import math

import jax
import jax.numpy as jnp
from jax import lax
from jax.experimental import pallas as pl
from jax.experimental.pallas import tpu as pltpu
from jax.sharding import PartitionSpec as P


PANELS = 3


def split(value):
    high = value.astype(jnp.bfloat16)
    low = (value - high.astype(jnp.float32)).astype(jnp.bfloat16)
    return high, low


def product(left, right):
    dot = functools.partial(jnp.dot, preferred_element_type=jnp.float32)
    return dot(left[0], right[0]) + (dot(left[0], right[1]) + dot(left[1], right[0]))


def invert(block):
    size = block.shape[0]
    eye = lax.broadcasted_iota(jnp.int32, (size, size), 0) == lax.broadcasted_iota(jnp.int32, (size, size), 1)
    diagonal = jnp.where(eye, block, 0.0)
    down = 1.0 / jnp.sum(diagonal, axis=1, keepdims=True)
    along = 1.0 / jnp.sum(diagonal, axis=0, keepdims=True)
    first = jnp.where(eye, 2.0 * down, 0.0) - down * block * along
    parts = split(first)
    inner = product(split(block), parts)
    return 2.0 * first - product(parts, split(inner))


def distance_groups(row_count):
    groups = []
    for distance in range(1, row_count):
        targets = {(k + distance) % row_count for k in range(PANELS)}
        for group in groups:
            if not targets & group[1]:
                group[0].append(distance)
                group[1].update(targets)
                break
        else:
            groups.append(([distance], targets))
    groups = [group[0] for group in groups]
    return groups[:1] + groups[2:], groups[1]


LANES = 128


def load(ref, index, size):
    step = size // LANES
    return jnp.concatenate([ref[(*index, pl.ds(part, size, stride=step), slice(None))] for part in range(step)], axis=1)


def store(ref, index, value):
    size = value.shape[0]
    step = size // LANES
    for part in range(step):
        ref[(*index, pl.ds(part, size, stride=step), slice(None))] = value[:, part * LANES : (part + 1) * LANES]


def plane_kinds(row_count):
    kinds = {}
    for plane in range(row_count):
        late = [k for k in range(PANELS) if (plane - k) % row_count in distance_groups(row_count)[1]]
        kinds.setdefault((late[0] if late else None, plane < PANELS), []).append(plane)
    return kinds


def column(index, size):
    return slice(index * size, (index + 1) * size)


def place(work, target, mine, other, piece, own, own_index):
    size = work.shape[1]
    even = lax.rem(lax.axis_index("pcol"), 2) == 0
    work[target, :, column(PANELS, size)] = load(own, (own_index,), size)

    @pl.when(even)
    def _():
        work[target, :, column(0, size)] = load(mine, (0, piece), size)
        work[target, :, column(1, size)] = load(other, (0, piece), size)
        work[target, :, column(2, size)] = load(mine, (1, piece), size)

    @pl.when(jnp.logical_not(even))
    def _():
        work[target, :, column(0, size)] = load(other, (0, piece), size)
        work[target, :, column(1, size)] = load(mine, (0, piece), size)
        work[target, :, column(2, size)] = load(other, (1, piece), size)


def place_arrived(work, group, mine, other, piece, own):
    my_row, row_count = lax.axis_index("prow"), lax.axis_size("prow")
    for distance in group:
        source = lax.rem(my_row + row_count - distance, row_count)

        @pl.when(source < PANELS)
        def _():
            place(work, source, mine, other, piece, own, piece)


def run_panel(work, panel, rows, begin=True):
    size = work.shape[1]
    if begin:
        inverse = invert(work[panel, :, column(panel, size)])
        work[panel, :, column(panel, size)] = inverse
    else:
        inverse = work[panel, :, column(panel, size)]
    inverse = split(inverse)
    rest = slice((panel + 1) * size, (PANELS + 1) * size)
    pivot_row = split(work[panel, :, rest])
    for index in rows:
        factor = product(split(work[index, :, column(panel, size)]), inverse)
        work[index, :, column(panel, size)] = factor
        work[index, :, rest] = work[index, :, rest] - product(split(factor), pivot_row)


def for_kinds(count, run):
    my_row = lax.axis_index("prow")
    for (late, own_pivot), planes in plane_kinds(lax.axis_size("prow")).items():
        here = functools.reduce(jnp.logical_or, [my_row == plane for plane in planes])
        own = range(PANELS + (1 if own_pivot else 0), PANELS + count)

        @pl.when(here)
        def _():
            run(late, list(own))


def early_kernel(tile, far, own_mine, own_other, far_mine, far_other, work):
    count = tile.shape[0]
    my_row = lax.axis_index("prow")
    for index in range(count):
        place(work, PANELS + index, own_mine, own_other, index, tile, index)

    @pl.when(my_row < PANELS)
    def _():
        place(work, my_row, own_mine, own_other, 0, tile, 0)

    for number, group in enumerate(distance_groups(lax.axis_size("prow"))[0]):
        place_arrived(work, group, far_mine, far_other, number, far)

    def run(late, own):
        if late != 0:
            run_panel(work, 0, [index for index in range(1, PANELS) if index != late] + own)

    for_kinds(count, run)


def late_kernel(near, near_mine, near_other, given, out, work):
    del given
    size, count = work.shape[1], work.shape[0] - PANELS
    my_row, my_col = lax.axis_index("prow"), lax.axis_index("pcol")
    place_arrived(work, distance_groups(lax.axis_size("prow"))[1], near_mine, near_other, 0, near)

    def run(late, own):
        if late == 0:
            run_panel(work, 0, [*range(1, PANELS), *own])
        elif late is not None:
            run_panel(work, 0, [late], begin=False)
        for panel in range(1, PANELS):
            run_panel(work, panel, [*range(panel + 1, PANELS), *own])

    for_kinds(count, run)
    at = jnp.where(my_col < PANELS, my_col, PANELS)
    columns = pl.ds(pl.multiple_of(at * size, size), size)
    first = jnp.where(my_row < PANELS, my_row, PANELS)
    store(out, (0,), work[first, :, columns])
    for index in range(1, count):
        store(out, (index,), work[PANELS + index, :, columns])


def in_vmem(kernel, out_shapes, operands, spare=4, aliases={}):
    words = sum(operand.size for operand in operands) + sum(math.prod(shape) for shape in out_shapes)
    return pl.pallas_call(
        kernel,
        out_shape=[jax.ShapeDtypeStruct(shape, jnp.float32) for shape in out_shapes],
        in_specs=[pl.BlockSpec(memory_space=pltpu.VMEM)] * len(operands),
        out_specs=[pl.BlockSpec(memory_space=pltpu.VMEM)] * len(out_shapes),
        input_output_aliases=aliases,
        compiler_params=pltpu.CompilerParams(vmem_limit_bytes=4 * words + spare * 1024 * 1024),
    )(*operands)


def reverse(mask, chips):
    bits = chips.bit_length() - 1
    return sum(((mask >> bit) & 1) << (bits - 1 - bit) for bit in range(bits))


def pick_kernel(*refs):
    sources, mine = refs[:-1], refs[-1]
    chips = len(sources)
    me = lax.axis_index("pcol")
    even = lax.rem(me, 2) == 0
    for chip in range(chips):

        @pl.when(jnp.logical_and(me // 2 == chip, even))
        def _():
            mine[0] = sources[chip][...]
            mine[1] = sources[chip ^ 1][...]

        @pl.when(jnp.logical_and(me // 2 == chip, jnp.logical_not(even)))
        def _():
            mine[0] = sources[reverse(chip, chips)][...]


def arrivals(block):
    chips = lax.axis_size("pcol") // 2
    arrived = {0: block}

    def chip_of(column, mask):
        return column // 2 ^ (reverse(mask, chips) if column % 2 else mask)

    for mask in sorted(range(1, chips), key=lambda mask: (mask.bit_count(), -mask)):
        before = mask & (mask - 1)
        arrived[mask] = lax.ppermute(
            arrived[before],
            "pcol",
            [(2 * chip_of(c, before) + c % 2, 2 * chip_of(c, mask) + c % 2) for c in range(PANELS)],
        )
    return [arrived[mask] for mask in sorted(arrived)]


def exchange(arrived):
    (mine,) = in_vmem(pick_kernel, [(2, *arrived[0].shape)], arrived)
    other = lax.ppermute(mine, "pcol", [(c, c ^ 1) for c in range(lax.axis_size("pcol"))])
    return mine, other


def factored(matrix):
    shape = matrix.shape
    size = shape[4]
    tile = matrix.reshape(shape[0], shape[2] * size // LANES, LANES)
    row_count = lax.axis_size("prow")
    far_groups, near_group = distance_groups(row_count)

    def from_rows(block, group):
        total = None
        for d in group:
            arrived = lax.ppermute(block, "prow", [(k, (k + d) % row_count) for k in range(PANELS)])
            total = arrived if total is None else total + arrived
        return total

    rows = [from_rows(tile[:1], group) for group in far_groups]
    own = arrivals(tile)
    late, first = lax.optimization_barrier((tile[:1], rows[0]))
    near = from_rows(late, near_group)
    far = jnp.concatenate([first] + rows[1:])
    own = exchange(own)
    far_arrived = exchange(arrivals(far))
    near_arrived = exchange(arrivals(near))
    work = (PANELS + shape[0], size, (PANELS + 1) * size)
    (done,) = in_vmem(early_kernel, [work], [tile, far, *own, *far_arrived], 16)
    result, _ = in_vmem(late_kernel, [tile.shape, work], [near, *near_arrived, done], 16, {3: 1})
    return result.reshape(shape)


def solution(mesh):
    return jax.shard_map(
        factored,
        mesh=mesh,
        in_specs=(P(None, "prow", None, "pcol", None),),
        out_specs=P(None, "prow", None, "pcol", None),
        check_vma=False,
    )
```

```python
import functools
import math

import jax
import jax.numpy as jnp
from jax import lax
from jax.experimental import pallas as pl
from jax.experimental.pallas import tpu as pltpu
from jax.sharding import PartitionSpec as P


PANELS = 3


def split(value):
    high = value.astype(jnp.bfloat16)
    low = (value - high.astype(jnp.float32)).astype(jnp.bfloat16)
    return high, low


def product(left, right):
    dot = functools.partial(jnp.dot, preferred_element_type=jnp.float32)
    return dot(left[0], right[0]) + (dot(left[0], right[1]) + dot(left[1], right[0]))


def invert(block):
    size = block.shape[0]
    eye = lax.broadcasted_iota(jnp.int32, (size, size), 0) == lax.broadcasted_iota(jnp.int32, (size, size), 1)
    diagonal = jnp.where(eye, block, 0.0)
    down = 1.0 / jnp.sum(diagonal, axis=1, keepdims=True)
    along = 1.0 / jnp.sum(diagonal, axis=0, keepdims=True)
    first = jnp.where(eye, 2.0 * down, 0.0) - down * block * along
    parts = split(first)
    inner = product(split(block), parts)
    return 2.0 * first - product(parts, split(inner))


def distance_groups(row_count):
    groups = []
    for distance in range(1, row_count):
        targets = {(k + distance) % row_count for k in range(PANELS)}
        for group in groups:
            if not targets & group[1]:
                group[0].append(distance)
                group[1].update(targets)
                break
        else:
            groups.append(([distance], targets))
    groups = [group[0] for group in groups]
    return groups[:1] + groups[2:], groups[1]


LANES = 128


def load(ref, index, size):
    step = size // LANES
    return jnp.concatenate([ref[(*index, pl.ds(part, size, stride=step), slice(None))] for part in range(step)], axis=1)


def store(ref, index, value):
    size = value.shape[0]
    step = size // LANES
    for part in range(step):
        ref[(*index, pl.ds(part, size, stride=step), slice(None))] = value[:, part * LANES : (part + 1) * LANES]


def comes_late(row, plane, row_count):
    distance = (plane - row) % row_count
    return distance in distance_groups(row_count)[1] and (distance != 2 or row + 2 < row_count)


def plane_kinds(row_count):
    kinds = {}
    for plane in range(row_count):
        late = [k for k in range(PANELS) if comes_late(k, plane, row_count)]
        kinds.setdefault((late[0] if late else None, plane < PANELS), []).append(plane)
    return kinds


def column(index, size):
    return slice(index * size, (index + 1) * size)


def place(work, target, mine, other, piece, own, own_index):
    size = work.shape[1]
    even = lax.rem(lax.axis_index("pcol"), 2) == 0
    work[target, :, column(PANELS, size)] = load(own, (own_index,), size)

    @pl.when(even)
    def _():
        work[target, :, column(0, size)] = load(mine, (0, piece), size)
        work[target, :, column(1, size)] = load(other, (0, piece), size)
        work[target, :, column(2, size)] = load(mine, (1, piece), size)

    @pl.when(jnp.logical_not(even))
    def _():
        work[target, :, column(0, size)] = load(other, (0, piece), size)
        work[target, :, column(1, size)] = load(mine, (0, piece), size)
        work[target, :, column(2, size)] = load(other, (1, piece), size)


def place_arrived(work, group, mine, other, piece, own, late):
    my_row, row_count = lax.axis_index("prow"), lax.axis_size("prow")
    for distance in group:
        source = lax.rem(my_row + row_count - distance, row_count)
        here = source < PANELS
        if distance == 2:
            here = jnp.logical_and(here, (source + 2 < row_count) == late)

        @pl.when(here)
        def _():
            place(work, source, mine, other, piece, own, piece)


def run_panel(work, panel, rows, begin=True):
    size = work.shape[1]
    if begin:
        inverse = invert(work[panel, :, column(panel, size)])
        work[panel, :, column(panel, size)] = inverse
    else:
        inverse = work[panel, :, column(panel, size)]
    inverse = split(inverse)
    rest = slice((panel + 1) * size, (PANELS + 1) * size)
    pivot_row = split(work[panel, :, rest])
    for index in rows:
        factor = product(split(work[index, :, column(panel, size)]), inverse)
        work[index, :, column(panel, size)] = factor
        work[index, :, rest] = work[index, :, rest] - product(split(factor), pivot_row)


def for_kinds(count, run):
    my_row = lax.axis_index("prow")
    for (late, own_pivot), planes in plane_kinds(lax.axis_size("prow")).items():
        here = functools.reduce(jnp.logical_or, [my_row == plane for plane in planes])
        own = range(PANELS + (1 if own_pivot else 0), PANELS + count)

        @pl.when(here)
        def _():
            run(late, list(own))


def early_kernel(tile, far, own_mine, own_other, far_mine, far_other, work):
    count = tile.shape[0]
    my_row = lax.axis_index("prow")
    for index in range(count):
        place(work, PANELS + index, own_mine, own_other, index, tile, index)

    @pl.when(my_row < PANELS)
    def _():
        place(work, my_row, own_mine, own_other, 0, tile, 0)

    for number, group in enumerate(distance_groups(lax.axis_size("prow"))[0]):
        place_arrived(work, group + [2] * (number == 0), far_mine, far_other, number, far, False)

    def run(late, own):
        if late != 0:
            run_panel(work, 0, [index for index in range(1, PANELS) if index != late] + own)

    for_kinds(count, run)


def late_kernel(near, near_mine, near_other, given, out, work):
    del given
    size, count = work.shape[1], work.shape[0] - PANELS
    my_row, my_col = lax.axis_index("prow"), lax.axis_index("pcol")
    place_arrived(work, distance_groups(lax.axis_size("prow"))[1], near_mine, near_other, 0, near, True)

    def run(late, own):
        if late == 0:
            run_panel(work, 0, [*range(1, PANELS), *own])
        elif late is not None:
            run_panel(work, 0, [late], begin=False)
        for panel in range(1, PANELS):
            run_panel(work, panel, [*range(panel + 1, PANELS), *own])

    for_kinds(count, run)
    at = jnp.where(my_col < PANELS, my_col, PANELS)
    columns = pl.ds(pl.multiple_of(at * size, size), size)
    first = jnp.where(my_row < PANELS, my_row, PANELS)
    store(out, (0,), work[first, :, columns])
    for index in range(1, count):
        store(out, (index,), work[PANELS + index, :, columns])


def in_vmem(kernel, out_shapes, operands, spare=4, aliases={}):
    words = sum(operand.size for operand in operands) + sum(math.prod(shape) for shape in out_shapes)
    return pl.pallas_call(
        kernel,
        out_shape=[jax.ShapeDtypeStruct(shape, jnp.float32) for shape in out_shapes],
        in_specs=[pl.BlockSpec(memory_space=pltpu.VMEM)] * len(operands),
        out_specs=[pl.BlockSpec(memory_space=pltpu.VMEM)] * len(out_shapes),
        input_output_aliases=aliases,
        compiler_params=pltpu.CompilerParams(vmem_limit_bytes=4 * words + spare * 1024 * 1024),
    )(*operands)


def reverse(mask, chips):
    bits = chips.bit_length() - 1
    return sum(((mask >> bit) & 1) << (bits - 1 - bit) for bit in range(bits))


def pick_kernel(*refs):
    sources, mine = refs[:-1], refs[-1]
    chips = len(sources)
    me = lax.axis_index("pcol")
    even = lax.rem(me, 2) == 0
    for chip in range(chips):

        @pl.when(jnp.logical_and(me // 2 == chip, even))
        def _():
            mine[0] = sources[chip][...]
            mine[1] = sources[chip ^ 1][...]

        @pl.when(jnp.logical_and(me // 2 == chip, jnp.logical_not(even)))
        def _():
            mine[0] = sources[reverse(chip, chips)][...]


def arrivals(block, planes):
    chips = lax.axis_size("pcol") // 2
    arrived = {0: block}

    def chip_of(column, mask):
        return column // 2 ^ (reverse(mask, chips) if column % 2 else mask)

    for mask in sorted(range(1, chips), key=lambda mask: (mask.bit_count(), -mask)):
        before = mask & (mask - 1)
        pairs = [(2 * chip_of(c, before) + c % 2, 2 * chip_of(c, mask) + c % 2) for c in range(PANELS)]
        arrived[mask] = lax.ppermute(
            arrived[before],
            ("prow", "pcol"),
            [(p * 2 * chips + a, p * 2 * chips + b) for p in planes for a, b in pairs],
        )
    return [arrived[mask] for mask in sorted(arrived)]


def exchange(arrived):
    (mine,) = in_vmem(pick_kernel, [(2, *arrived[0].shape)], arrived)
    other = lax.ppermute(mine, "pcol", [(c, c ^ 1) for c in range(lax.axis_size("pcol"))])
    return mine, other


def factored(matrix):
    shape = matrix.shape
    size = shape[4]
    tile = matrix.reshape(shape[0], shape[2] * size // LANES, LANES)
    row_count = lax.axis_size("prow")
    far_groups, near_group = distance_groups(row_count)

    def from_rows(block, pairs):
        return lax.ppermute(block, "prow", pairs)

    def total(parts):
        return functools.reduce(jnp.add, parts)

    def direct(d):
        return from_rows(tile[:1], [(k, (k + d) % row_count) for k in range(PANELS)])

    next_row = direct(1)
    rows = [[direct(d) for d in group if d != 1] for group in far_groups]
    rows[0].append(next_row)
    wrapped = [(k, (k + 2) % row_count) for k in range(PANELS) if k + 2 >= row_count]
    if wrapped:
        rows[0].append(from_rows(tile[:1], wrapped))
    far = jnp.concatenate([total(parts) for parts in rows])
    passed = from_rows(next_row, [(k + 1, k + 2) for k in range(PANELS) if k + 2 < row_count])
    near = total([passed] + [direct(d) for d in near_group if d != 2])
    every = range(row_count)
    late_planes = [p for p in every if any(comes_late(k, p, row_count) for k in range(PANELS))]
    own = exchange(arrivals(tile, every))
    far_arrived = exchange(arrivals(far, every))
    near_arrived = exchange(arrivals(near, late_planes))
    work = (PANELS + shape[0], size, (PANELS + 1) * size)
    (done,) = in_vmem(early_kernel, [work], [tile, far, *own, *far_arrived], 16)
    result, _ = in_vmem(late_kernel, [tile.shape, work], [near, *near_arrived, done], 16, {3: 1})
    return result.reshape(shape)


def solution(mesh):
    return jax.shard_map(
        factored,
        mesh=mesh,
        in_specs=(P(None, "prow", None, "pcol", None),),
        out_specs=P(None, "prow", None, "pcol", None),
        check_vma=False,
    )
```
